128 devices in a mesh: replica: 16 (over z, y), tensor: 8 (over x, core).
Axes of the slice: x: 4, y: 4, z: 4, core: 2. Of those that a mesh axis runs over, the one named last changes fastest.
Arguments:
- attended: bfloat16 [16384, 8192], P('replica', 'tensor'), may hold values from -6 to 6
- out_weight: bfloat16 [8192, 8192], P('tensor'), may hold values from -0.09375 to 0.09375
- shrink_weight: bfloat16 [192, 64, 8192], P('replica', None, 'tensor'), may hold values from -0.0625 to 0.0625
- expand_weight: bfloat16 [192, 64, 8192], P('replica', None, 'tensor'), may hold values from -0.75 to 0.75
- block_adapter: int32 [128], P('replica'), may hold values from 0 to 191, as said below
- block_fill: int32 [128], P('replica'), may hold values from 1 to 128
Outputs:
- projected: bfloat16 [16384, 8192], P('replica', 'tensor')
The draws below stay inside these ranges and needn't reach their ends.
Inputs may be any that keep to these rules, and one draw needn't show every extreme that they name: `block_adapter`: the owner of adapter j is replica j // 12. Among the 8 blocks of one replica, at most 1 have adapters of one owner; one owner gets exactly 1 block from every replica.
All inputs are finite; a program needn't handle non-finite values.
Results may differ from the reference program's by a relative error of at most 0.02.
Values may be sent and summed in bfloat16 or wider, within the bound.
No kernel may reach another device: no remote copies, remote signals or barrier semaphores. Data moves between devices by JAX's collectives and lax.ppermute only.
A program may use at most 128 MiB of HBM per device.

```python
import jax
import jax.numpy as jnp
from jax import lax

D = 8192
RANK = 64
BLOCK = 128
BLK_DEV = 8
CAP = 1
ADP_REP = 12
TOKENS = 16384
BLOCKS = 128
ADAPTERS = 192
N_TENSOR = 8


def draw_block_adapter(key, part):
    owner_count = ADAPTERS // ADP_REP
    replica_count = BLOCKS // BLK_DEV
    hot_key, rest_key = jax.random.split(jax.random.fold_in(key, 7))
    hot_rank = jax.random.permutation(hot_key, owner_count)
    replica_keys = jax.random.split(rest_key, replica_count)
    if CAP > 1:
        lowest = max(1, (BLK_DEV - owner_count + CAP - 2) // (CAP - 1))
    else:
        lowest = 1
    highest = max(lowest + 1, BLK_DEV // CAP + 1)

    def one_replica(replica_key):
        score_key, double_key, within_key = jax.random.split(replica_key, 3)
        scores = jax.random.randint(score_key, (owner_count,), 0, 4 * owner_count)
        scores = scores + jnp.where(hot_rank == 0, 8 * owner_count, 0) + jnp.where(hot_rank == 1, 3 * owner_count, 0)
        distinct = scores * owner_count + jnp.arange(owner_count)
        order = jnp.argsort(-distinct)
        doubles = jax.random.randint(double_key, (), lowest, highest)
        positions = jnp.arange(BLK_DEV)
        pattern = jnp.where(positions < CAP * doubles, positions // CAP, doubles + positions - CAP * doubles)
        owner_of = order[pattern]
        within = jax.random.randint(within_key, (BLK_DEV,), 0, ADP_REP)
        return owner_of * ADP_REP + within
    return jax.vmap(one_replica)(replica_keys).reshape(BLOCKS).astype(jnp.int32)


def touch_ends(entries, stream_key, low, largest):
    extent = entries.shape
    place = [jax.random.randint(jax.random.fold_in(stream_key, axis), (), 0, extent[axis]) for axis in range(len(extent))]
    entries = entries.at[tuple(place)].set(low)
    longest = extent.index(max(extent))
    place[longest] = (place[longest] + 1) % extent[longest]
    return entries.at[tuple(place)].set(largest)


def with_spikes(values, own_key, source, target, blocks, factor):
    def block_of(dim):
        return (jnp.arange(values.shape[dim]) // (values.shape[dim] // blocks)).reshape((-1,) + (1,) * (values.ndim - 1 - dim))

    one_side = jax.random.permutation(own_key, blocks)[block_of(target)]
    other_side = (block_of(target) + blocks // 2) % blocks
    return jnp.where((block_of(source) == one_side) | (block_of(source) == other_side), factor * values, values)


def level_of(key, extent, cuts, smallest, largest):
    factor_of, own = 1.0, jax.random.fold_in(key, 6)
    for axis_at, parts in cuts:
        steps = jnp.exp(jax.random.uniform(jax.random.fold_in(own, axis_at), (parts,), jnp.float32, smallest / len(cuts), largest / len(cuts)))
        factor_of = factor_of * jnp.repeat(steps, extent[axis_at] // parts).reshape([-1 if axis == axis_at else 1 for axis in range(len(extent))])
    return factor_of


def bell_draw(rng, dims, width, bound, cuts=(), kind=jnp.bfloat16):
    drawn = width * jax.random.normal(rng, dims, jnp.float32)
    if cuts:
        drawn = drawn * level_of(rng, dims, cuts, -0.22, 0.18)
    return jnp.clip(drawn, -bound, bound).astype(kind)


def noise_with(own_key, dims, width, most, shards, heavy, held_as=jnp.bfloat16):
    result = width * jax.random.normal(own_key, dims, jnp.float32)
    if shards:
        result = result * level_of(own_key, dims, shards, -0.22, 0.18)
    return jnp.clip(with_spikes(result, jax.random.fold_in(own_key, 3), *heavy), -most, most).astype(held_as)


def setup_inputs(seed: int = 0) -> dict:
    seeds = jax.random.split(jax.random.key(seed), 7)
    attended = bell_draw(seeds[0], (TOKENS, D), 1.0, 6.0, ((0, 16), (1, 8)))
    out_weight = noise_with(seeds[1], (D, D), D ** -0.5, 0.09375, ((0, 8),), (0, 1, 8, 2.0))
    shrink_weight = bell_draw(seeds[2], (ADAPTERS, RANK, D), D ** -0.5, 0.0625, ((0, 16), (2, 8)))
    expand_weight = bell_draw(seeds[3], (ADAPTERS, RANK, D), RANK ** -0.5, 0.75, ((0, 16), (2, 8)))
    block_adapter = draw_block_adapter(jax.random.fold_in(seeds[6], 71), 0)
    block_fill = touch_ends(jax.random.randint(seeds[5], (BLOCKS,), 1, BLOCK + 1), jax.random.fold_in(seeds[5], 1), 1, BLOCK).astype(jnp.int32)
    return dict(attended=attended, out_weight=out_weight, shrink_weight=shrink_weight, expand_weight=expand_weight, block_adapter=block_adapter, block_fill=block_fill)


def reference(attended, out_weight, shrink_weight, expand_weight, block_adapter, block_fill):
    feature_piece = D // N_TENSOR
    base_out = jnp.zeros((TOKENS, D), jnp.float32)
    for shard_index in range(N_TENSOR):
        columns = attended[:, shard_index * feature_piece:(shard_index + 1) * feature_piece]
        weight_rows = out_weight[shard_index * feature_piece:(shard_index + 1) * feature_piece, :]
        partial_out = jnp.dot(columns, weight_rows, preferred_element_type=jnp.float32).astype(jnp.bfloat16)
        partial_out = lax.optimization_barrier(partial_out)
        base_out = base_out + partial_out.astype(jnp.float32)
    block_count = TOKENS // BLOCK
    row_blocks = attended.reshape(block_count, BLOCK, D).astype(jnp.float32)
    shrink_sel = shrink_weight[block_adapter].astype(jnp.float32)
    low_rank = jnp.einsum("bcd,brd->bcr", row_blocks, shrink_sel).astype(jnp.bfloat16)
    low_rank = lax.optimization_barrier(low_rank)
    expand_sel = expand_weight[block_adapter].astype(jnp.float32)
    delta_rows = jnp.einsum("bcr,brd->bcd", low_rank.astype(jnp.float32), expand_sel).astype(jnp.bfloat16)
    delta_rows = lax.optimization_barrier(delta_rows)
    combined = base_out.reshape(block_count, BLOCK, D) + delta_rows.astype(jnp.float32)
    live_rows = jnp.arange(BLOCK, dtype=jnp.int32)[None, :] < block_fill[:, None]
    projected = jnp.where(live_rows[:, :, None], combined, 0.0).astype(jnp.bfloat16)
    return projected.reshape(TOKENS, D)
```

```python
import functools

import jax
import jax.numpy as jnp
from jax import lax
from jax.experimental import pallas as pl
from jax.experimental.pallas import tpu as pltpu
from jax.sharding import PartitionSpec as P

BN = 512
IDS = 1
COST = pl.CostEstimate(flops=10_000_000_000, bytes_accessed=10_000_000, transcendentals=0)


def any_spec():
    return pl.BlockSpec(memory_space=pl.ANY)


def in_hbm(a):
    return pltpu.with_memory_space_constraint(a, pltpu.HBM)


def params():
    return pltpu.CompilerParams(vmem_limit_bytes=20 * 1024 * 1024)


def choose(values, k):
    out = values[-1]
    for i in range(len(values) - 2, -1, -1):
        out = jnp.where(k == i, values[i], out) if values[i] is not out else out
    return out


def clamp(g, steps, k):
    return jnp.clip(g - k * steps, 0, steps - 1)


def tasks_kernel(tasks, steps, sched, a_ref, ap_ref, w_ref, *refs):
    n = len(tasks)
    others, adds, outs = refs[:n], refs[n:], refs[-n:]
    at = 0
    for k, count in enumerate(tasks):
        mine = adds[at:at + count]
        at += count

        @pl.when(pl.program_id(0) // steps == k)
        def _(k=k, mine=mine):
            acc = jnp.dot(a_ref[...], w_ref[...], preferred_element_type=jnp.float32)
            acc = acc + jnp.dot(ap_ref[...], others[k][...], preferred_element_type=jnp.float32)
            for add in mine:
                acc = acc + add[...].astype(jnp.float32)
            outs[k][...] = acc.astype(outs[k].dtype)


def matmuls(sched, att, att_other, weight, rows, tasks, deps=()):
    width = att.shape[1]
    depth = weight.shape[0]
    steps = width // BN

    def a_map(g, s):
        return (choose([t[1] // rows for t in tasks], g // steps), 0)

    def w_map(g, s):
        slot = choose([t[0] for t in tasks], g // steps)
        return (0, s[slot] * steps + g % steps)

    in_specs = [pl.BlockSpec((rows, width), a_map), pl.BlockSpec((rows, width), a_map), pl.BlockSpec((depth, BN), w_map)]
    operands = [att, att_other, weight]
    for k, task in enumerate(tasks):
        array, row = task[2]
        in_specs.append(pl.BlockSpec((depth, BN), lambda g, s, k=k, row=row: (row // depth, clamp(g, steps, k))))
        operands.append(array)
    for k, task in enumerate(tasks):
        for array, row in task[3]:
            in_specs.append(pl.BlockSpec((rows, BN), lambda g, s, k=k, row=row: (row // rows, clamp(g, steps, k))))
            operands.append(array)
    in_specs += [any_spec() for _ in deps]
    return pl.pallas_call(
        functools.partial(tasks_kernel, [len(t[3]) for t in tasks], steps),
        grid_spec=pltpu.PrefetchScalarGridSpec(
            num_scalar_prefetch=1,
            grid=(steps * len(tasks),),
            in_specs=in_specs,
            out_specs=[pl.BlockSpec((rows, BN), lambda g, s, k=k: (0, clamp(g, steps, k))) for k in range(len(tasks))],
        ),
        out_shape=[pltpu.HBM((rows, width), jnp.bfloat16) for _ in tasks],
        compiler_params=params(),
        cost_estimate=COST,
    )(sched, *[in_hbm(a) for a in operands], *[in_hbm(a) for a in deps])


def shrink_kernel(blocks, rows, adapters, a_ref, *refs):
    o_ref = refs[-1]
    for b in range(blocks):
        o_ref[b] = lax.dot_general(
            refs[b][0], a_ref[b * rows:(b + 1) * rows, :], (((1,), (1,)), ((), ())), preferred_element_type=jnp.float32
        ).astype(o_ref.dtype)


def shrink(adapters, att, slots, per_owner, deps=()):
    blocks = adapters.shape[0]
    rows = att.shape[0] // blocks
    _, rank, width = slots.shape
    in_specs = [pl.BlockSpec(att.shape, lambda g, ad: (0, 0))]
    for b in range(blocks):
        in_specs.append(pl.BlockSpec((1, rank, width), lambda g, ad, b=b: (ad[b] // per_owner, 0, 0)))
    in_specs += [any_spec() for _ in deps]
    return pl.pallas_call(
        functools.partial(shrink_kernel, blocks, rows),
        grid_spec=pltpu.PrefetchScalarGridSpec(
            num_scalar_prefetch=1,
            grid=(1,),
            in_specs=in_specs,
            out_specs=pl.BlockSpec((blocks, rank, rows), lambda g, ad: (0, 0, 0)),
        ),
        out_shape=jax.ShapeDtypeStruct((blocks, rank, rows), jnp.bfloat16),
        compiler_params=params(),
        cost_estimate=COST,
    )(adapters, in_hbm(att), *([in_hbm(slots)] * blocks), *[in_hbm(a) for a in deps])


def final_kernel(per, n_low, sched, adapters, fill, a_ref, ap_ref, w_ref, wp_ref, *refs):
    pairs, refs = refs[:4], refs[4:]
    lows, refs = refs[:n_low], refs[n_low:]
    expands, o_ref = refs[:2 * per], refs[-1]
    rows = a_ref.shape[0]
    block = rows // per
    for k in range(2):

        @pl.when(pl.program_id(0) == k)
        def _(k=k):
            base = jnp.dot(a_ref[...], w_ref[...], preferred_element_type=jnp.float32)
            base = base + jnp.dot(ap_ref[...], wp_ref[...], preferred_element_type=jnp.float32)
            for add in (pairs[2 * k], pairs[2 * k + 1]):
                base = base + add[...].astype(jnp.float32)
            for i in range(per):
                b = k * per + i
                low = lows[0][b].astype(jnp.float32)
                for other in lows[1:]:
                    low = low + other[b].astype(jnp.float32)
                delta = lax.dot_general(
                    low.astype(jnp.bfloat16), expands[b][0], (((0,), (0,)), ((), ())), preferred_element_type=jnp.float32
                ).astype(jnp.bfloat16)
                out = base[i * block:(i + 1) * block] + delta.astype(jnp.float32)
                live = lax.broadcasted_iota(jnp.int32, out.shape, 0) < fill[b]
                o_ref[i * block:(i + 1) * block, :] = jnp.where(live, out, 0.0).astype(o_ref.dtype)


def finish(sched, adapters, fill, att, att_other, weight, weight_other, pairs, lows, expand_slots, per_owner):
    blocks = adapters.shape[0]
    tokens, width = att.shape
    rows = tokens // 2
    steps = width // BN
    per = blocks // 2
    rank = expand_slots.shape[1]
    in_specs = [
        pl.BlockSpec((rows, width), lambda k, j, s, ad, fl: (k, 0)),
        pl.BlockSpec((rows, width), lambda k, j, s, ad, fl: (k, 0)),
        pl.BlockSpec((weight.shape[0], BN), lambda k, j, s, ad, fl: (0, s[0] * steps + j)),
        pl.BlockSpec((weight.shape[0], BN), lambda k, j, s, ad, fl: (0, j)),
    ]
    for k0 in range(2):
        for _ in range(2):
            in_specs.append(
                pl.BlockSpec((rows, BN), lambda k, j, s, ad, fl, k0=k0: (0, clamp(k * steps + j, steps, k0)))
            )
    for low in lows:
        in_specs.append(pl.BlockSpec(low.shape, lambda k, j, s, ad, fl: (0, 0, 0)))
    for b in range(blocks):
        in_specs.append(pl.BlockSpec((1, rank, BN), lambda k, j, s, ad, fl, b=b: (ad[b] // per_owner, 0, j)))
    return pl.pallas_call(
        functools.partial(final_kernel, per, len(lows)),
        grid_spec=pltpu.PrefetchScalarGridSpec(
            num_scalar_prefetch=3,
            grid=(2, steps),
            in_specs=in_specs,
            out_specs=pl.BlockSpec((rows, BN), lambda k, j, s, ad, fl: (k, j)),
        ),
        out_shape=jax.ShapeDtypeStruct(att.shape, jnp.bfloat16),
        compiler_params=params(),
        cost_estimate=COST,
    )(sched, adapters, fill, *[in_hbm(a) for a in (att, att_other, weight, weight_other, *pairs, *lows, *([expand_slots] * blocks))])


def after(a, *others):
    return lax.optimization_barrier((a, *others))[0]


def local(attended, out_weight, shrink_weight, expand_weight, block_adapter, block_fill):
    tokens, width = attended.shape
    owners = lax.axis_size("replica")
    n_tensor = lax.axis_size("tensor")
    chips = n_tensor // 2
    per_owner = shrink_weight.shape[0]
    half = tokens // 2
    t = lax.axis_index("tensor")
    x, c = t >> 1, t & 1

    i8 = jnp.arange(2 * chips, dtype=jnp.int32)
    sched = 2 * ((x + (i8 >> 1)) % chips) + ((c + i8) & 1)

    def send(a, chip_step):
        pairs = [(s, (s + 2 * chip_step) % n_tensor) for s in range(n_tensor)]
        return lax.ppermute(a, "tensor", pairs)

    def swap(a):
        return lax.ppermute(a, "tensor", [(s, s ^ 1) for s in range(n_tensor)])

    def exchange(a):
        return lax.all_to_all(a, "replica", 0, 0, tiled=True)

    OPP, NEXT, PREV, OWN = 4, 2, 6, 0

    owner_of = block_adapter // per_owner
    wanted = jnp.where(jnp.arange(owners)[:, None] == owner_of[None, :], (block_adapter - owner_of * per_owner)[None, :], 0)
    request = jnp.broadcast_to(jnp.sum(wanted, axis=1)[:, None, None], (owners, IDS, 128)).astype(jnp.int32)

    def lend(k):
        return swap(lax.dynamic_slice_in_dim(out_weight, sched[k + 1] * width, width, axis=1))

    att_other = swap(attended)
    opp_other = lend(OPP)
    served = exchange(request)[:, 0, 0]
    mm = functools.partial(matmuls, sched, attended, att_other, out_weight, half)

    opp_a, opp_b = mm([(OPP, 0, (opp_other, 0), ()), (OPP, half, (opp_other, 0), ())])
    right_1, left_1 = send(opp_a, 1), send(opp_b, -1)

    shrink_slots = exchange(shrink_weight[served])
    expand_slots = exchange(expand_weight[served])

    next_other, prev_other = lend(NEXT), lend(PREV)
    next_b, prev_a = mm([(NEXT, half, (next_other, 0), ()), (PREV, 0, (prev_other, 0), ())], deps=(opp_a,))
    next_b = after(next_b, right_1, left_1)
    right_2, left_2 = send(next_b, 1), send(prev_a, -1)
    next_a, prev_b = mm(
        [(NEXT, 0, (next_other, 0), ((right_1, 0),)), (PREV, half, (prev_other, 0), ((left_1, 0),))], deps=(next_b,)
    )
    own_other = lend(OWN)

    part = shrink(block_adapter, attended, shrink_slots, per_owner, deps=(next_a,))
    chip = (part.astype(jnp.float32) + swap(part).astype(jnp.float32)).astype(jnp.bfloat16)
    lows = [chip] + [send(chip, k) for k in range(1, chips)]

    next_a, prev_b, _, _ = lax.optimization_barrier((next_a, prev_b, right_2, left_2))
    right_3, left_3 = send(next_a, 1), send(prev_b, -1)

    pairs = (right_3, left_2, left_3, right_2)
    return finish(
        sched, block_adapter, block_fill, attended, att_other, out_weight, own_other, pairs, lows, expand_slots, per_owner
    )


def solution(mesh):
    in_specs = (
        P("replica", "tensor"),
        P("tensor", None),
        P("replica", None, "tensor"),
        P("replica", None, "tensor"),
        P("replica"),
        P("replica"),
    )
    out_specs = P("replica", "tensor")
    return jax.shard_map(local, mesh=mesh, in_specs=in_specs, out_specs=out_specs, check_vma=False)
```

```python
import functools

import jax
import jax.numpy as jnp
from jax import lax
from jax.experimental import pallas as pl
from jax.experimental.pallas import tpu as pltpu
from jax.sharding import PartitionSpec as P

BN = 512
IDS = 1
COST = pl.CostEstimate(flops=10000000000,bytes_accessed=10000000, transcendentals=0)


def any_spec():
    return pl.BlockSpec(memory_space=pl.ANY)


def in_hbm(a):
    return pltpu.with_memory_space_constraint(a, pltpu.HBM)


def params():
    return pltpu.CompilerParams(vmem_limit_bytes=20 * 1024 * 1024)


def choose(values, k):
    out = values[-1]
    for i in range(len(values) - 2, -1, -1):
        out = jnp.where(k == i, values[i], out) if values[i] is not out else out
    return out


def clamp(g, steps, k):
    return jnp.clip(g - k * steps, 0, steps - 1)


def tasks_kernel(tasks, steps, sched, a_ref, ap_ref, w_ref, wp_ref, *refs):
    n = len(tasks)
    outs = refs[-n:]
    at = 0
    for k, count in enumerate(tasks):
        mine = refs[at:at + count]
        at += count

        @pl.when(pl.program_id(0) // steps == k)
        def _(k=k, mine=mine):
            acc = jnp.dot(a_ref[...], w_ref[...], preferred_element_type=jnp.float32)
            acc = acc + jnp.dot(ap_ref[...], wp_ref[...], preferred_element_type=jnp.float32)
            for add in mine:
                acc = acc + add[...].astype(jnp.float32)
            outs[k][...] = acc.astype(outs[k].dtype)


def matmuls(sched, att, att_other, weight, weight_other, rows, tasks, deps=()):
    width = att.shape[1]
    depth = weight.shape[0]
    steps = width // BN
    alone = weight_other.shape[1] == width

    def a_map(g, s):
        return (choose([t[1] // rows for t in tasks], g // steps), 0)

    def w_map(g, s):
        slot = choose([t[0] for t in tasks], g // steps)
        return (0, s[slot] * steps + g % steps)

    in_specs = [
        pl.BlockSpec((rows, width), a_map),
        pl.BlockSpec((rows, width), a_map),
        pl.BlockSpec((depth, BN), w_map),
        pl.BlockSpec((depth, BN), (lambda g, s: (0, g % steps)) if alone else w_map),
    ]
    operands = [att, att_other, weight, weight_other]
    for k, task in enumerate(tasks):
        for array, row in task[2]:
            in_specs.append(pl.BlockSpec((rows, BN), lambda g, s, k=k, row=row: (row // rows, clamp(g, steps, k))))
            operands.append(array)
    in_specs += [any_spec() for _ in deps]
    return pl.pallas_call(
        functools.partial(tasks_kernel, [len(t[2]) for t in tasks], steps),
        grid_spec=pltpu.PrefetchScalarGridSpec(
            num_scalar_prefetch=1,
            grid=(steps * len(tasks),),
            in_specs=in_specs,
            out_specs=[pl.BlockSpec((rows, BN), lambda g, s, k=k: (0, clamp(g, steps, k))) for k in range(len(tasks))],
        ),
        out_shape=[pltpu.HBM((rows, width), jnp.bfloat16) for _ in tasks],
        compiler_params=params(),
        cost_estimate=COST,
    )(sched, *[in_hbm(a) for a in operands], *[in_hbm(a) for a in deps])


def shrink_kernel(blocks, rows, adapters, a_ref, *refs):
    o_ref = refs[-1]
    for b in range(blocks):
        o_ref[b] = lax.dot_general(
            refs[b][0], a_ref[b * rows:(b + 1) * rows, :], (((1,), (1,)), ((), ())), preferred_element_type=jnp.float32
        ).astype(o_ref.dtype)


def shrink(adapters, att, slots, per_owner, deps=()):
    blocks = adapters.shape[0]
    rows = att.shape[0] // blocks
    _, rank, width = slots.shape
    in_specs = [pl.BlockSpec(att.shape, lambda g, ad: (0, 0))]
    for b in range(blocks):
        in_specs.append(pl.BlockSpec((1, rank, width), lambda g, ad, b=b: (ad[b] // per_owner, 0, 0)))
    in_specs += [any_spec() for _ in deps]
    return pl.pallas_call(
        functools.partial(shrink_kernel, blocks, rows),
        grid_spec=pltpu.PrefetchScalarGridSpec(
            num_scalar_prefetch=1,
            grid=(1,),
            in_specs=in_specs,
            out_specs=pl.BlockSpec((blocks, rank, rows), lambda g, ad: (0, 0, 0)),
        ),
        out_shape=jax.ShapeDtypeStruct((blocks, rank, rows), jnp.bfloat16),
        compiler_params=params(),
        cost_estimate=COST,
    )(adapters, in_hbm(att), *([in_hbm(slots)] * blocks), *[in_hbm(a) for a in deps])


def final_kernel(per, n_low, adapters, fill, *refs):
    parts, refs = refs[:4], refs[4:]
    lows, refs = refs[:n_low], refs[n_low:]
    expands, o_ref = refs[:2 * per], refs[-1]
    block = parts[0].shape[0] // per
    for k in range(2):

        @pl.when(pl.program_id(0) == k)
        def _(k=k):
            for i in range(per):
                b = k * per + i
                rows = slice(i * block, (i + 1) * block)
                low = lows[0][b].astype(jnp.float32)
                for other in lows[1:]:
                    low = low + other[b].astype(jnp.float32)
                delta = lax.dot_general(
                    low.astype(jnp.bfloat16), expands[b][0], (((0,), (0,)), ((), ())), preferred_element_type=jnp.float32
                ).astype(jnp.bfloat16)
                base = parts[2 * k][rows, :].astype(jnp.float32) + parts[2 * k + 1][rows, :].astype(jnp.float32)
                out = base + delta.astype(jnp.float32)
                live = lax.broadcasted_iota(jnp.int32, out.shape, 0) < fill[b]
                o_ref[rows, :] = jnp.where(live, out, 0.0).astype(o_ref.dtype)


def finish(adapters, fill, parts, lows, expand_slots, per_owner):
    blocks = adapters.shape[0]
    rows, width = parts[0].shape
    steps = width // BN
    per = blocks // 2
    rank = expand_slots.shape[1]
    in_specs = []
    for k0 in range(2):
        for _ in range(2):
            in_specs.append(pl.BlockSpec((rows, BN), lambda k, j, ad, fl, k0=k0: (0, clamp(k * steps + j, steps, k0))))
    for low in lows:
        in_specs.append(pl.BlockSpec(low.shape, lambda k, j, ad, fl: (0, 0, 0)))
    for b in range(blocks):
        in_specs.append(
            pl.BlockSpec(
                (1, rank, BN),
                lambda k, j, ad, fl, b=b: (ad[b] // per_owner, 0, clamp(k * steps + j, steps, b // per)),
            )
        )
    return pl.pallas_call(
        functools.partial(final_kernel, per, len(lows)),
        grid_spec=pltpu.PrefetchScalarGridSpec(
            num_scalar_prefetch=2,
            grid=(2, steps),
            in_specs=in_specs,
            out_specs=pl.BlockSpec((rows, BN), lambda k, j, ad, fl: (k, j)),
        ),
        out_shape=jax.ShapeDtypeStruct((2 * rows, width), jnp.bfloat16),
        compiler_params=params(),
        cost_estimate=COST,
    )(adapters, fill, *[in_hbm(a) for a in (*parts, *lows, *([expand_slots] * blocks))])


def after(a, *others):
    return lax.optimization_barrier((a, *others))[0]


def local(attended, out_weight, shrink_weight, expand_weight, block_adapter, block_fill):
    tokens, width = attended.shape
    owners = lax.axis_size("replica")
    n_tensor = lax.axis_size("tensor")
    chips = n_tensor // 2
    per_owner = shrink_weight.shape[0]
    half = tokens // 2
    t = lax.axis_index("tensor")
    x, c = t >> 1, t & 1

    i8 = jnp.arange(2 * chips, dtype=jnp.int32)
    sched = 2 * ((x + (i8 >> 1)) % chips) + ((c + i8) & 1)

    def send(a, chip_step):
        pairs = [(s, (s + 2 * chip_step) % n_tensor) for s in range(n_tensor)]
        return lax.ppermute(a, "tensor", pairs)

    def swap(a):
        return lax.ppermute(a, "tensor", [(s, s ^ 1) for s in range(n_tensor)])

    def exchange(a):
        return lax.all_to_all(a, "replica", 0, 0, tiled=True)

    OPP, NEXT, PREV, OWN = 4, 2, 6, 0

    owner_of = block_adapter // per_owner
    wanted = jnp.where(jnp.arange(owners)[:, None] == owner_of[None, :], (block_adapter - owner_of * per_owner)[None, :], 0)
    request = jnp.broadcast_to(jnp.sum(wanted, axis=1)[:, None, None], (owners, IDS, 128)).astype(jnp.int32)

    att_other = swap(attended)
    start = (2 * lax.rem(x + OPP // 2, chips) + (1 - c)) * width
    opp_piece = lax.dynamic_slice_in_dim(out_weight, start, width, axis=1)
    opp_other = swap(opp_piece)
    asked = exchange(after(request, opp_piece))
    weight_other = swap(after(out_weight, opp_other, att_other))
    mm = functools.partial(matmuls, sched, attended, att_other, out_weight)

    opp_a, opp_b = mm(opp_other, half, [(OPP, 0, ()), (OPP, half, ())], deps=(asked,))
    right_1, left_1 = send(opp_a, 1), send(opp_b, -1)

    served = after(asked[:, 0, 0], opp_a)
    shrink_slots = exchange(shrink_weight[served])
    expand_slots = exchange(expand_weight[served])

    mm = functools.partial(mm, weight_other, half)
    next_b, prev_a = mm([(NEXT, half, ()), (PREV, 0, ())], deps=(opp_a,))
    right_2, left_2 = send(next_b, 1), send(prev_a, -1)
    next_a, prev_b = mm([(NEXT, 0, ((right_1, 0),)), (PREV, half, ((left_1, 0),))], deps=(next_b,))

    part = shrink(block_adapter, attended, shrink_slots, per_owner, deps=(next_a,))
    chip = (part.astype(jnp.float32) + swap(part).astype(jnp.float32)).astype(jnp.bfloat16)
    lows = [chip] + [send(chip, k) for k in range(1, chips)]

    next_a, prev_b, _, _ = lax.optimization_barrier((next_a, prev_b, right_2, left_2))
    right_3, left_3 = send(next_a, 1), send(prev_b, -1)

    own_a, own_b = mm([(OWN, 0, ((left_2, 0),)), (OWN, half, ((right_2, 0),))], deps=(next_a,))
    return finish(block_adapter, block_fill, (own_a, right_3, own_b, left_3), lows, expand_slots, per_owner)


def solution(mesh):
    in_specs = (
        P("replica", "tensor"),
        P("tensor", None),
        P("replica", None, "tensor"),
        P("replica", None, "tensor"),
        P("replica"),
        P("replica"),
    )
    out_specs = P("replica", "tensor")
    return jax.shard_map(local, mesh=mesh, in_specs=in_specs, out_specs=out_specs, check_vma=False)
```

```python
import functools

import jax
import jax.numpy as jnp
from jax import lax
from jax.experimental import pallas as pl
from jax.experimental.pallas import tpu as pltpu
from jax.sharding import PartitionSpec as P

BN = 512
FBN = 1024
IDS = 1
COST = pl.CostEstimate(flops=10000000000,bytes_accessed=10000000, transcendentals=0)


def any_spec():
    return pl.BlockSpec(memory_space=pl.ANY)


def in_hbm(a):
    return pltpu.with_memory_space_constraint(a, pltpu.HBM)


def params():
    return pltpu.CompilerParams(vmem_limit_bytes=20 * 1024 * 1024)


def choose(values, k):
    out = values[-1]
    for i in range(len(values) - 2, -1, -1):
        out = jnp.where(k == i, values[i], out) if values[i] is not out else out
    return out


def clamp(g, steps, k):
    return jnp.clip(g - k * steps, 0, steps - 1)


def tasks_kernel(tasks, steps, sched, a_ref, ap_ref, w_ref, wp_ref, *refs):
    n = len(tasks)
    outs = refs[-n:]
    at = 0
    for k, count in enumerate(tasks):
        mine = refs[at:at + count]
        at += count

        @pl.when(pl.program_id(0) // steps == k)
        def _(k=k, mine=mine):
            acc = jnp.dot(a_ref[...], w_ref[...], preferred_element_type=jnp.float32)
            acc = acc + jnp.dot(ap_ref[...], wp_ref[...], preferred_element_type=jnp.float32)
            for add in mine:
                acc = acc + add[...].astype(jnp.float32)
            outs[k][...] = acc.astype(outs[k].dtype)


def matmuls(sched, att, att_other, weight, weight_other, rows, tasks, deps=()):
    width = att.shape[1]
    depth = weight.shape[0]
    steps = width // BN
    alone = weight_other.shape[1] == width

    def a_map(g, s):
        return (choose([t[1] // rows for t in tasks], g // steps), 0)

    def w_map(g, s):
        slot = choose([t[0] for t in tasks], g // steps)
        return (0, s[slot] * steps + g % steps)

    in_specs = [
        pl.BlockSpec((rows, width), a_map),
        pl.BlockSpec((rows, width), a_map),
        pl.BlockSpec((depth, BN), w_map),
        pl.BlockSpec((depth, BN), (lambda g, s: (0, g % steps)) if alone else w_map),
    ]
    operands = [att, att_other, weight, weight_other]
    for k, task in enumerate(tasks):
        for array, row in task[2]:
            in_specs.append(pl.BlockSpec((rows, BN), lambda g, s, k=k, row=row: (row // rows, clamp(g, steps, k))))
            operands.append(array)
    in_specs += [any_spec() for _ in deps]
    return pl.pallas_call(
        functools.partial(tasks_kernel, [len(t[2]) for t in tasks], steps),
        grid_spec=pltpu.PrefetchScalarGridSpec(
            num_scalar_prefetch=1,
            grid=(steps * len(tasks),),
            in_specs=in_specs,
            out_specs=[pl.BlockSpec((rows, BN), lambda g, s, k=k: (0, clamp(g, steps, k))) for k in range(len(tasks))],
        ),
        out_shape=[pltpu.HBM((rows, width), jnp.bfloat16) for _ in tasks],
        compiler_params=params(),
        cost_estimate=COST,
    )(sched, *[in_hbm(a) for a in operands], *[in_hbm(a) for a in deps])


def shrink_kernel(blocks, rows, adapters, a_ref, *refs):
    o_ref = refs[-1]
    for b in range(blocks):
        o_ref[b] = lax.dot_general(
            refs[b][0], a_ref[b * rows:(b + 1) * rows, :], (((1,), (1,)), ((), ())), preferred_element_type=jnp.float32
        ).astype(o_ref.dtype)


def shrink(adapters, att, slots, per_owner, deps=()):
    blocks = adapters.shape[0]
    rows = att.shape[0] // blocks
    _, rank, width = slots.shape
    in_specs = [pl.BlockSpec(att.shape, lambda g, ad: (0, 0))]
    for b in range(blocks):
        in_specs.append(pl.BlockSpec((1, rank, width), lambda g, ad, b=b: (ad[b] // per_owner, 0, 0)))
    in_specs += [any_spec() for _ in deps]
    return pl.pallas_call(
        functools.partial(shrink_kernel, blocks, rows),
        grid_spec=pltpu.PrefetchScalarGridSpec(
            num_scalar_prefetch=1,
            grid=(1,),
            in_specs=in_specs,
            out_specs=pl.BlockSpec((blocks, rank, rows), lambda g, ad: (0, 0, 0)),
        ),
        out_shape=jax.ShapeDtypeStruct((blocks, rank, rows), jnp.bfloat16),
        compiler_params=params(),
        cost_estimate=COST,
    )(adapters, in_hbm(att), *([in_hbm(slots)] * blocks), *[in_hbm(a) for a in deps])


def final_kernel(per, n_low, adapters, fill, *refs):
    parts, refs = refs[:4], refs[4:]
    lows, refs = refs[:n_low], refs[n_low:]
    expands, o_ref = refs[:2 * per], refs[-1]
    block = parts[0].shape[0] // per
    for k in range(2):

        @pl.when(pl.program_id(0) == k)
        def _(k=k):
            for i in range(per):
                b = k * per + i
                rows = slice(i * block, (i + 1) * block)
                low = lows[0][b].astype(jnp.float32)
                for other in lows[1:]:
                    low = low + other[b].astype(jnp.float32)
                delta = lax.dot_general(
                    low.astype(jnp.bfloat16), expands[b][0], (((0,), (0,)), ((), ())), preferred_element_type=jnp.float32
                ).astype(jnp.bfloat16)
                base = parts[2 * k][rows, :].astype(jnp.float32) + parts[2 * k + 1][rows, :].astype(jnp.float32)
                out = base + delta.astype(jnp.float32)
                live = lax.broadcasted_iota(jnp.int32, out.shape, 0) < fill[b]
                o_ref[rows, :] = jnp.where(live, out, 0.0).astype(o_ref.dtype)


def finish(adapters, fill, parts, lows, expand_slots, per_owner):
    blocks = adapters.shape[0]
    rows, width = parts[0].shape
    steps = width // FBN
    per = blocks // 2
    rank = expand_slots.shape[1]
    in_specs = []
    for k0 in range(2):
        for _ in range(2):
            in_specs.append(pl.BlockSpec((rows, FBN), lambda k, j, ad, fl, k0=k0: (0, clamp(k * steps + j, steps, k0))))
    for low in lows:
        in_specs.append(pl.BlockSpec(low.shape, lambda k, j, ad, fl: (0, 0, 0)))
    for b in range(blocks):
        in_specs.append(
            pl.BlockSpec(
                (1, rank, FBN),
                lambda k, j, ad, fl, b=b: (ad[b] // per_owner, 0, clamp(k * steps + j, steps, b // per)),
            )
        )
    return pl.pallas_call(
        functools.partial(final_kernel, per, len(lows)),
        grid_spec=pltpu.PrefetchScalarGridSpec(
            num_scalar_prefetch=2,
            grid=(2, steps),
            in_specs=in_specs,
            out_specs=pl.BlockSpec((rows, FBN), lambda k, j, ad, fl: (k, j)),
        ),
        out_shape=jax.ShapeDtypeStruct((2 * rows, width), jnp.bfloat16),
        compiler_params=params(),
        cost_estimate=COST,
    )(adapters, fill, *[in_hbm(a) for a in (*parts, *lows, *([expand_slots] * blocks))])


def after(a, *others):
    return lax.optimization_barrier((a, *others))[0]


def local(attended, out_weight, shrink_weight, expand_weight, block_adapter, block_fill):
    tokens, width = attended.shape
    owners = lax.axis_size("replica")
    n_tensor = lax.axis_size("tensor")
    chips = n_tensor // 2
    per_owner = shrink_weight.shape[0]
    half = tokens // 2
    t = lax.axis_index("tensor")
    x, c = t >> 1, t & 1

    i8 = jnp.arange(2 * chips, dtype=jnp.int32)
    sched = 2 * ((x + (i8 >> 1)) % chips) + ((c + i8) & 1)

    def send(a, chip_step):
        pairs = [(s, (s + 2 * chip_step) % n_tensor) for s in range(n_tensor)]
        return lax.ppermute(a, "tensor", pairs)

    def swap(a):
        return lax.ppermute(a, "tensor", [(s, s ^ 1) for s in range(n_tensor)])

    def exchange(a):
        return lax.all_to_all(a, "replica", 0, 0, tiled=True)

    OPP, NEXT, PREV, OWN = 4, 2, 6, 0

    owner_of = block_adapter // per_owner
    wanted = jnp.where(jnp.arange(owners)[:, None] == owner_of[None, :], (block_adapter - owner_of * per_owner)[None, :], 0)
    request = jnp.broadcast_to(jnp.sum(wanted, axis=1)[:, None, None], (owners, IDS, 128)).astype(jnp.int32)

    att_other = swap(attended)
    start = (2 * lax.rem(x + OPP // 2, chips) + (1 - c)) * width
    opp_piece = lax.dynamic_slice_in_dim(out_weight, start, width, axis=1)
    opp_other = swap(opp_piece)
    asked = exchange(after(request, opp_piece))
    weight_other = swap(after(out_weight, opp_other, att_other))
    mm = functools.partial(matmuls, sched, attended, att_other, out_weight)

    opp_a, opp_b = mm(opp_other, half, [(OPP, 0, ()), (OPP, half, ())], deps=())
    right_1, left_1 = send(opp_a, 1), send(opp_b, -1)

    served = after(asked, opp_a)[:, 0, 0]
    shrink_slots = exchange(shrink_weight[served])
    expand_slots = exchange(expand_weight[served])

    mm = functools.partial(mm, weight_other, half)
    next_b, prev_a = mm([(NEXT, half, ()), (PREV, 0, ())], deps=(opp_a,))
    right_2, left_2 = send(next_b, 1), send(prev_a, -1)
    next_a, prev_b = mm([(NEXT, 0, ((right_1, 0),)), (PREV, half, ((left_1, 0),))], deps=(next_b,))

    part = shrink(block_adapter, attended, shrink_slots, per_owner, deps=(next_a,))
    chip = (part.astype(jnp.float32) + swap(part).astype(jnp.float32)).astype(jnp.bfloat16)
    lows = [chip] + [send(chip, k) for k in range(1, chips)]

    next_a, prev_b, _, _ = lax.optimization_barrier((next_a, prev_b, right_2, left_2))
    right_3, left_3 = send(next_a, 1), send(prev_b, -1)

    own_a, own_b = mm([(OWN, 0, ((left_2, 0),)), (OWN, half, ((right_2, 0),))], deps=(next_a,))
    return finish(block_adapter, block_fill, (own_a, right_3, own_b, left_3), lows, expand_slots, per_owner)


def solution(mesh):
    in_specs = (
        P("replica", "tensor"),
        P("tensor", None),
        P("replica", None, "tensor"),
        P("replica", None, "tensor"),
        P("replica"),
        P("replica"),
    )
    out_specs = P("replica", "tensor")
    return jax.shard_map(local, mesh=mesh, in_specs=in_specs, out_specs=out_specs, check_vma=False)
```

```python
import functools

import jax
import jax.numpy as jnp
from jax import lax
from jax.experimental import pallas as pl
from jax.experimental.pallas import tpu as pltpu
from jax.sharding import PartitionSpec as P

BN = 512
FBN = 1024
IDS = 1
COST = pl.CostEstimate(flops=10000000000,bytes_accessed=10000000, transcendentals=0)


def any_spec():
    return pl.BlockSpec(memory_space=pl.ANY)


def in_hbm(a):
    return pltpu.with_memory_space_constraint(a, pltpu.HBM)


def params():
    return pltpu.CompilerParams(vmem_limit_bytes=20 * 1024 * 1024)


def choose(values, k):
    out = values[-1]
    for i in range(len(values) - 2, -1, -1):
        out = jnp.where(k == i, values[i], out) if values[i] is not out else out
    return out


def clamp(g, steps, k):
    return jnp.clip(g - k * steps, 0, steps - 1)


def tasks_kernel(tasks, steps, sched, a_ref, ap_ref, w_ref, wp_ref, *refs):
    n = len(tasks)
    outs = refs[-n:]
    at = 0
    for k, count in enumerate(tasks):
        mine = refs[at:at + count]
        at += count

        @pl.when(pl.program_id(0) // steps == k)
        def _(k=k, mine=mine):
            acc = jnp.dot(a_ref[...], w_ref[...], preferred_element_type=jnp.float32)
            acc = acc + jnp.dot(ap_ref[...], wp_ref[...], preferred_element_type=jnp.float32)
            for add in mine:
                acc = acc + add[...].astype(jnp.float32)
            outs[k][...] = acc.astype(outs[k].dtype)


def matmuls(sched, att, att_other, weight, weight_other, rows, tasks, deps=()):
    width = att.shape[1]
    depth = weight.shape[0]
    steps = width // BN
    alone = weight_other.shape[1] == width

    def a_map(g, s):
        return (choose([t[1] // rows for t in tasks], g // steps), 0)

    def w_map(g, s):
        slot = choose([t[0] for t in tasks], g // steps)
        return (0, s[slot] * steps + g % steps)

    in_specs = [
        pl.BlockSpec((rows, width), a_map),
        pl.BlockSpec((rows, width), a_map),
        pl.BlockSpec((depth, BN), w_map),
        pl.BlockSpec((depth, BN), (lambda g, s: (0, g % steps)) if alone else w_map),
    ]
    operands = [att, att_other, weight, weight_other]
    for k, task in enumerate(tasks):
        for array, row in task[2]:
            in_specs.append(pl.BlockSpec((rows, BN), lambda g, s, k=k, row=row: (row // rows, clamp(g, steps, k))))
            operands.append(array)
    in_specs += [any_spec() for _ in deps]
    return pl.pallas_call(
        functools.partial(tasks_kernel, [len(t[2]) for t in tasks], steps),
        grid_spec=pltpu.PrefetchScalarGridSpec(
            num_scalar_prefetch=1,
            grid=(steps * len(tasks),),
            in_specs=in_specs,
            out_specs=[pl.BlockSpec((rows, BN), lambda g, s, k=k: (0, clamp(g, steps, k))) for k in range(len(tasks))],
        ),
        out_shape=[pltpu.HBM((rows, width), jnp.bfloat16) for _ in tasks],
        compiler_params=params(),
        cost_estimate=COST,
    )(sched, *[in_hbm(a) for a in operands], *[in_hbm(a) for a in deps])


def shrink_kernel(blocks, rows, adapters, a_ref, *refs):
    o_ref = refs[-1]
    for b in range(blocks):
        o_ref[b] = lax.dot_general(
            refs[b][0], a_ref[b * rows:(b + 1) * rows, :], (((1,), (1,)), ((), ())), preferred_element_type=jnp.float32
        ).astype(o_ref.dtype)


def shrink(adapters, att, slots, per_owner, deps=()):
    blocks = adapters.shape[0]
    rows = att.shape[0] // blocks
    _, rank, width = slots.shape
    in_specs = [pl.BlockSpec(att.shape, lambda g, ad: (0, 0))]
    for b in range(blocks):
        in_specs.append(pl.BlockSpec((1, rank, width), lambda g, ad, b=b: (ad[b] // per_owner, 0, 0)))
    in_specs += [any_spec() for _ in deps]
    return pl.pallas_call(
        functools.partial(shrink_kernel, blocks, rows),
        grid_spec=pltpu.PrefetchScalarGridSpec(
            num_scalar_prefetch=1,
            grid=(1,),
            in_specs=in_specs,
            out_specs=pl.BlockSpec((blocks, rank, rows), lambda g, ad: (0, 0, 0)),
        ),
        out_shape=jax.ShapeDtypeStruct((blocks, rank, rows), jnp.bfloat16),
        compiler_params=params(),
        cost_estimate=COST,
    )(adapters, in_hbm(att), *([in_hbm(slots)] * blocks), *[in_hbm(a) for a in deps])


def final_kernel(per, n_low, adapters, fill, *refs):
    parts, refs = refs[:4], refs[4:]
    lows, refs = refs[:n_low], refs[n_low:]
    expands, o_ref = refs[:2 * per], refs[-1]
    block = parts[0].shape[0] // per
    for k in range(2):

        @pl.when(pl.program_id(0) == k)
        def _(k=k):
            for i in range(per):
                b = k * per + i
                rows = slice(i * block, (i + 1) * block)
                low = lows[0][b].astype(jnp.float32)
                for other in lows[1:]:
                    low = low + other[b].astype(jnp.float32)
                delta = lax.dot_general(
                    low.astype(jnp.bfloat16), expands[b][0], (((0,), (0,)), ((), ())), preferred_element_type=jnp.float32
                ).astype(jnp.bfloat16)
                base = parts[2 * k][rows, :].astype(jnp.float32) + parts[2 * k + 1][rows, :].astype(jnp.float32)
                out = base + delta.astype(jnp.float32)
                live = lax.broadcasted_iota(jnp.int32, out.shape, 0) < fill[b]
                o_ref[rows, :] = jnp.where(live, out, 0.0).astype(o_ref.dtype)


def finish(adapters, fill, parts, lows, expand_slots, per_owner):
    blocks = adapters.shape[0]
    rows, width = parts[0].shape
    steps = width // FBN
    per = blocks // 2
    rank = expand_slots.shape[1]
    in_specs = []
    for k0 in range(2):
        for _ in range(2):
            in_specs.append(pl.BlockSpec((rows, FBN), lambda k, j, ad, fl, k0=k0: (0, clamp(k * steps + j, steps, k0))))
    for low in lows:
        in_specs.append(pl.BlockSpec(low.shape, lambda k, j, ad, fl: (0, 0, 0)))
    for b in range(blocks):
        in_specs.append(
            pl.BlockSpec(
                (1, rank, FBN),
                lambda k, j, ad, fl, b=b: (ad[b] // per_owner, 0, clamp(k * steps + j, steps, b // per)),
            )
        )
    return pl.pallas_call(
        functools.partial(final_kernel, per, len(lows)),
        grid_spec=pltpu.PrefetchScalarGridSpec(
            num_scalar_prefetch=2,
            grid=(2, steps),
            in_specs=in_specs,
            out_specs=pl.BlockSpec((rows, FBN), lambda k, j, ad, fl: (k, j)),
        ),
        out_shape=jax.ShapeDtypeStruct((2 * rows, width), jnp.bfloat16),
        compiler_params=params(),
        cost_estimate=COST,
    )(adapters, fill, *[in_hbm(a) for a in (*parts, *lows, *([expand_slots] * blocks))])


def after(a, *others):
    return lax.optimization_barrier((a, *others))[0]


def local(attended, out_weight, shrink_weight, expand_weight, block_adapter, block_fill):
    tokens, width = attended.shape
    owners = lax.axis_size("replica")
    n_tensor = lax.axis_size("tensor")
    chips = n_tensor // 2
    per_owner = shrink_weight.shape[0]
    half = tokens // 2
    t = lax.axis_index("tensor")
    x, c = t >> 1, t & 1

    i8 = jnp.arange(2 * chips, dtype=jnp.int32)
    sched = 2 * ((x + (i8 >> 1)) % chips) + ((c + i8) & 1)

    def send(a, chip_step):
        pairs = [(s, (s + 2 * chip_step) % n_tensor) for s in range(n_tensor)]
        return lax.ppermute(a, "tensor", pairs)

    def swap(a):
        return lax.ppermute(a, "tensor", [(s, s ^ 1) for s in range(n_tensor)])

    def exchange(a):
        return lax.all_to_all(a, "replica", 0, 0, tiled=True)

    OPP, NEXT, PREV, OWN = 4, 2, 6, 0

    owner_of = block_adapter // per_owner
    wanted = jnp.where(jnp.arange(owners)[:, None] == owner_of[None, :], (block_adapter - owner_of * per_owner)[None, :], 0)
    request = jnp.broadcast_to(jnp.sum(wanted, axis=1)[:, None, None], (owners, IDS, 128)).astype(jnp.int32)

    att_other = swap(attended)
    start = (2 * lax.rem(x + OPP // 2, chips) + (1 - c)) * width
    opp_piece = lax.dynamic_slice_in_dim(out_weight, start, width, axis=1)
    opp_other = swap(opp_piece)
    asked = exchange(after(request, opp_piece))
    weight_other = swap(after(out_weight, opp_other, att_other))
    mm = functools.partial(matmuls, sched, attended, att_other, out_weight)

    opp_a, opp_b = mm(opp_other, half, [(OPP, 0, ()), (OPP, half, ())], deps=())
    right_1, left_1 = send(opp_a, 1), send(opp_b, -1)

    served = after(asked, opp_a)[:, 0, 0]
    shrink_slots = exchange(shrink_weight[served])
    expand_slots = exchange(expand_weight[served])

    mm = functools.partial(mm, weight_other, half)
    next_b, prev_a = mm([(NEXT, half, ()), (PREV, 0, ())], deps=(opp_a,))
    right_2, left_2 = send(next_b, 1), send(prev_a, -1)
    next_a, prev_b = mm([(NEXT, 0, ((right_1, 0),)), (PREV, half, ((left_1, 0),))], deps=(next_b,))

    part = shrink(block_adapter, attended, shrink_slots, per_owner, deps=(next_a,))
    chip = (part.astype(jnp.float32) + swap(part).astype(jnp.float32)).astype(jnp.bfloat16)
    lows = [chip] + [send(chip, k) for k in range(1, chips)]


    right_3, left_3 = send(next_a, 1), send(prev_b, -1)

    own_a, own_b = mm([(OWN, 0, ((left_2, 0),)), (OWN, half, ((right_2, 0),))], deps=(next_a,))
    return finish(block_adapter, block_fill, (own_a, right_3, own_b, left_3), lows, expand_slots, per_owner)


def solution(mesh):
    in_specs = (
        P("replica", "tensor"),
        P("tensor", None),
        P("replica", None, "tensor"),
        P("replica", None, "tensor"),
        P("replica"),
        P("replica"),
    )
    out_specs = P("replica", "tensor")
    return jax.shard_map(local, mesh=mesh, in_specs=in_specs, out_specs=out_specs, check_vma=False)
```
